32 devices in a mesh: frame: 4 (over x, core), cam: 8 (over z, y).
Axes of the slice: x: 2, y: 2, z: 4, core: 2. Of those that a mesh axis runs over, the one named last changes fastest.
Arguments:
- view_maps: bfloat16 [8, 88, 2, 32, 256], P('frame', 'cam'), may hold values from -6 to 6
- conv_weight: bfloat16 [9, 256, 256], replicated, may hold values from -0.125 to 0.125
- join_weight: bfloat16 [16384, 256], P('cam'), may hold values from -0.1875 to 0.1875
- valid_cams: int32 [8, 88], P('frame'), may hold values from 0 to 1, as said below
- latent_grad: bfloat16 [8, 256], P('frame'), may hold values from -6 to 6
Outputs:
- latent: float32 [8, 256], P('frame')
- conv_grad: float32 [9, 256, 256], replicated
- join_grad: float32 [16384, 256], P(('cam', 'frame'))
The draws below stay inside these ranges and needn't reach their ends.
Inputs may be any that keep to these rules, and one draw needn't show every extreme that they name: `valid_cams`: every frame has at least one usable camera; the last 6 cameras are padding and never usable.
All inputs are finite; a program needn't handle non-finite values.
Results may differ from the reference program's by a relative error of at most 0.007.
Values may be sent and summed in bfloat16 or wider, within the bound.
A program may use at most 64 MiB of HBM per device.

```python
import jax
import jax.numpy as jnp
from jax import lax

CH = 256
LAT = 256
COLS = 32
ROWS = 2
FRAMES = 8
CAMS = 88
FEAT = 16384


def draw_valid_cams(key, part):
    coin_key = jax.random.fold_in(key, 11)
    pick_key = jax.random.fold_in(key, 23)
    coins = jax.random.randint(coin_key, (FRAMES, CAMS), 0, 4)
    cam_index = jnp.arange(CAMS, dtype=jnp.int32)[None, :]
    usable = jnp.logical_and(coins > 0, cam_index < CAMS - 6)
    forced = jax.random.randint(pick_key, (FRAMES, 1), 0, CAMS - 6)
    chosen = jnp.logical_or(usable, cam_index == forced)
    return chosen.astype(jnp.int32)


def level_of(rng, extent, cuts, least, top_value):
    level, own = 1.0, jax.random.fold_in(rng, 6)
    for dim, parts in cuts:
        draws = jnp.exp(jax.random.uniform(jax.random.fold_in(own, dim), (parts,), jnp.float32, least / len(cuts), top_value / len(cuts)))
        level = level * jnp.repeat(draws, extent[dim] // parts).reshape([-1 if axis == dim else 1 for axis in range(len(extent))])
    return level


def gaussian(stream_key, shape, width, reach, shards=(), kind=jnp.bfloat16):
    array = jax.random.normal(stream_key, shape, jnp.float32) * width
    if len(shards) > 0:
        array = level_of(stream_key, shape, shards, -0.22, 0.18) * array
    return jnp.clip(array, min=-reach, max=reach).astype(kind)


def setup_inputs(seed: int = 0) -> dict:
    seeds = jax.random.split(jax.random.key(seed), 6)
    return {
        "view_maps": gaussian(seeds[0], (FRAMES, CAMS, ROWS, COLS, CH), 1.0, 6.0, ((0, 4), (1, 8))),
        "conv_weight": gaussian(seeds[1], (9, CH, CH), (9 * CH) ** -0.5, 0.125),
        "join_weight": gaussian(seeds[2], (FEAT, LAT), (FEAT // 16) ** -0.5, 0.1875, ((0, 8),)),
        "valid_cams": draw_valid_cams(jax.random.fold_in(seeds[5], 71), 0),
        "latent_grad": gaussian(seeds[4], (FRAMES, LAT), 1.0, 6.0, ((0, 4),)),
    }


def make_shifts(maps):
    padded = jnp.pad(maps, ((0, 0), (1, 1), (1, 1), (0, 0)))
    return [padded[:, dy:dy + ROWS, dx:dx + COLS, :].reshape(-1, CH) for dy in range(3) for dx in range(3)]


def reference(view_maps, conv_weight, join_weight, valid_cams, latent_grad):
    def frame_step(carry, inputs):
        conv_acc, join_acc = carry
        maps, valid_row, grad_row = inputs
        shifted = make_shifts(maps)
        preact = jnp.zeros((CAMS * ROWS * COLS, CH), jnp.float32)
        for k in range(9):
            preact = preact + jnp.dot(shifted[k], conv_weight[k], preferred_element_type=jnp.float32)
        sigma = jax.nn.sigmoid(preact)
        features = (preact * sigma).astype(jnp.bfloat16).reshape(CAMS, FEAT)
        mask_f = valid_row.astype(jnp.float32)
        cam_count = jnp.sum(mask_f)
        pooled = jnp.sum(mask_f[:, None] * features.astype(jnp.float32), axis=0)
        joined = (pooled / cam_count).astype(jnp.bfloat16)
        latent_row = jnp.dot(joined, join_weight, preferred_element_type=jnp.float32)
        joined_grad = jnp.dot(join_weight, grad_row, preferred_element_type=jnp.float32).astype(jnp.bfloat16)
        slopes = (sigma * (1.0 + preact * (1.0 - sigma))).reshape(CAMS, FEAT)
        weighting = mask_f / cam_count
        pre_grad = (joined_grad.astype(jnp.float32)[None, :] * weighting[:, None] * slopes).astype(jnp.bfloat16)
        pre_grad = pre_grad.reshape(-1, CH)
        taps = jnp.stack([jnp.dot(shifted[k].T, pre_grad, preferred_element_type=jnp.float32) for k in range(9)])
        conv_acc = conv_acc + taps
        join_acc = join_acc + jnp.outer(joined.astype(jnp.float32), grad_row.astype(jnp.float32))
        return (conv_acc, join_acc), latent_row

    start_carry = (jnp.zeros((9, CH, CH), jnp.float32), jnp.zeros((FEAT, LAT), jnp.float32))
    (conv_grad, join_grad), latent = lax.scan(frame_step, start_carry, (view_maps, valid_cams, latent_grad))
    return latent, conv_grad, join_grad
```

```python
import functools

import jax
import jax.numpy as jnp
from jax import lax
from jax.experimental import pallas as pl
from jax.experimental.pallas import tpu as pltpu
from jax.sharding import PartitionSpec as P

MESH = pl.DeviceIdType.MESH
LANES = 128


def step_kernel(plan, *refs):
    (F, C, n_x, n_y, n_z, u_a, u_b, n_f, n_c, n_w, ch, k) = plan
    (mask_s, wgt_s, cnt_s, x_ref, w_ref, jw_ref, jg_ref, cot_ref,
     o_ref, lat_ref, jall_ref, call_ref,
     z_ref, p_ref, sl_ref, g_ref, jgall, jgf, pool_own, pool_rcv, part, sc, rc, t_ref,
     r1a, r1b, r2a, r2b, r3a, r3b, jn_ref, lp_ref, latall,
     s_jg, v_jg, s_ct, v_ct, s_pl, v_pl, s_jn, v_jn, s_lt, v_lt, s_co, v_co,
     s_rs, v_rs, s_ag, v_ag) = refs
    f_me, c_me = lax.axis_index("frame"), lax.axis_index("cam")
    core, x_me = lax.rem(f_me, 2), f_me // 2
    y_me, z_me = lax.rem(c_me, n_y), c_me // n_y
    rows_f = n_c * n_w
    n = n_x * n_y * n_z
    a_rows = n * u_a
    pending = []

    def send(src, dst, ss, rs, where):
        copy = pltpu.make_async_remote_copy(
            src_ref=src, dst_ref=dst, send_sem=ss, recv_sem=rs,
            device_id=where, device_id_type=MESH)
        copy.start()
        pending.append(copy)
        return copy

    barrier = pltpu.get_barrier_semaphore()
    for off in range(1, C):
        pl.semaphore_signal(barrier, inc=1, device_id={"cam": lax.rem(c_me + off, C)}, device_id_type=MESH)
    for off in range(1, F):
        pl.semaphore_signal(barrier, inc=1, device_id={"frame": lax.rem(f_me + off, F)}, device_id_type=MESH)
    pl.semaphore_wait(barrier, C + F - 2)

    jg_cp, ct_cp = [], []
    for off in range(1, C):
        jg_cp.append(send(jg_ref, jgall.at[c_me], s_jg.at[off - 1], v_jg.at[off - 1],
                          {"cam": lax.rem(c_me + off, C)}))
    for off in range(1, F):
        ct_cp.append(send(cot_ref, call_ref.at[f_me], s_ct.at[off - 1], v_ct.at[off - 1],
                          {"frame": lax.rem(f_me + off, F)}))
    jgall[c_me] = jg_ref[...]
    call_ref[f_me] = cot_ref[...]

    col = lax.rem(lax.broadcasted_iota(jnp.int32, (rows_f, ch), 0), n_w)
    for f in range(n_f):
        for r in range(2):
            xb = x_ref[f, :, r].reshape(rows_f, ch)
            xf = xb.astype(jnp.float32)
            lo = jnp.where(col == 0, 0.0, pltpu.roll(xf, 1, 0)).astype(jnp.bfloat16)
            hi = jnp.where(col == n_w - 1, 0.0, pltpu.roll(xf, rows_f - 1, 0)).astype(jnp.bfloat16)
            rows = pl.ds(f * rows_f, rows_f)
            for dx, piece in enumerate((lo, xb, hi)):
                z_ref[rows, pl.ds((r * 3 + dx) * ch, ch)] = piece

    def forward(i, carry):
        f, r = i // 2, lax.rem(i, 2)
        row0 = pl.multiple_of(f * rows_f, 16)
        w0 = pl.multiple_of((1 - r) * 3 * ch, 256)
        p_ref[...] = jnp.dot(z_ref[pl.ds(row0, rows_f)], w_ref[pl.ds(w0, 6 * ch)],
                             preferred_element_type=jnp.float32)
        total = jnp.zeros((n_w, ch), jnp.float32)
        for c in range(n_c):
            pre = p_ref[pl.ds(c * n_w, n_w)]
            sig = jax.nn.sigmoid(pre)
            feat = (pre * sig).astype(jnp.bfloat16).astype(jnp.float32)
            total = total + mask_s[f, c] * feat
            sl_ref[f, r, pl.ds(c * n_w, n_w)] = wgt_s[f, c] * (sig * (1.0 + pre * (1.0 - sig)))
        pool_tmp = total
        jgf[f, pl.ds(pl.multiple_of(r * n_w, n_w), n_w)] = pool_tmp
        return carry

    lax.fori_loop(0, 2 * n_f, forward, 0)
    for c in range(C):
        for f in range(n_f):
            pool_own[c, f] = jgf[f, c * k:(c + 1) * k]
    pl_cp = []
    for off in range(1, C):
        to = lax.rem(c_me + off, C)
        pl_cp.append(send(pool_own.at[to], pool_rcv.at[off - 1], s_pl.at[off - 1], v_pl.at[off - 1], {"cam": to}))

    for cp in jg_cp:
        cp.wait_recv()
    for c in range(C):
        for f in range(n_f):
            jgf[f, c * k:(c + 1) * k] = jgall[c, f].astype(jnp.float32)
    for f in range(n_f):
        for r in range(2):
            jg = jgf[f, r * n_w:(r + 1) * n_w]
            for c in range(n_c):
                g = (jg * sl_ref[f, r, pl.ds(c * n_w, n_w)]).astype(jnp.bfloat16)
                g_ref[r, pl.ds(f * rows_f + c * n_w, n_w)] = g

    def dot_t(lane0, r):
        return lax.dot_general(z_ref[:, lane0:lane0 + 3 * ch], g_ref[r], (((0,), (0,)), ((), ())),
                               preferred_element_type=jnp.float32)

    third = 3 * ch
    spare = part.shape[1] - 3 * third
    if spare:
        part[:, 3 * third:] = jnp.zeros((2, spare, LANES), jnp.float32)
    co_cp = []
    for b in range(3):
        if b == 0:
            val = dot_t(0, 1)
        elif b == 1:
            val = dot_t(0, 0) + dot_t(third, 1)
        else:
            val = dot_t(third, 0)
        rows = pl.ds(b * third, third)
        part[0, rows] = val[:, :LANES]
        part[1, rows] = val[:, LANES:]
        sc[rows] = part[1 - core, rows].astype(jnp.bfloat16)
        co_cp.append(send(sc.at[rows], rc.at[rows], s_co.at[b], v_co.at[b], {"frame": f_me + 1 - 2 * core}))

    dig = {"x": (n_x, x_me, lambda v: {"frame": v * 2 + core}),
           "y": (n_y, y_me, lambda v: {"cam": z_me * n_y + v}),
           "z": (n_z, z_me, lambda v: {"cam": v * n_y + y_me})}
    halves = []
    sem_at = 0
    for base, u, order, bufs in ((0, u_a, "xyz", (r1a, r2a, r3a)), (a_rows, u_b, "yxz", (r1b, r2b, r3b))):
        start, size, stages = base, n * u, []
        for name, buf in zip(order, bufs):
            cnt, me, where = dig[name]
            size = size // cnt
            stages.append((start, size, cnt, me, where, buf, sem_at))
            start = start + me * size
            sem_at += cnt - 1
        halves.append((stages, start, u))

    def rs_send(stage):
        start, size, cnt, me, where, buf, s0 = stage
        out = []
        for off in range(1, cnt):
            v = lax.rem(me + off, cnt)
            rows = pl.ds(pl.multiple_of(start + v * size, 16), size)
            t_ref[rows] = part[core, rows].astype(jnp.bfloat16)
            out.append(send(t_ref.at[rows], buf.at[off - 1], s_rs.at[s0 + off - 1], v_rs.at[s0 + off - 1], where(v)))
        return out

    def rs_recv(stage, cps):
        start, size, cnt, me, where, buf, s0 = stage
        rows = pl.ds(pl.multiple_of(start + me * size, 16), size)
        acc = part[core, rows]
        for off, cp in enumerate(cps):
            cp.wait_recv()
            acc = acc + buf[off].astype(jnp.float32)
        part[core, rows] = acc

    third_of = [0, third, 2 * third, 3 * third]
    done = 0
    first = []
    for h, (base, rows_n) in enumerate(((0, a_rows), (a_rows, n * u_b))):
        while done < 3 and (h == 1 or third_of[done] < base + rows_n):
            co_cp[done].wait_recv()
            rows = pl.ds(done * third, third)
            part[core, rows] = part[core, rows] + rc[rows].astype(jnp.float32)
            done += 1
        first.append(rs_send(halves[h][0][0]))
    for cp in pl_cp:
        cp.wait_recv()
    pooled = pool_own[c_me]
    for off in range(C - 1):
        pooled = pooled + pool_rcv[off]
    lat = jnp.zeros((n_f, jw_ref.shape[1]), jnp.float32)
    for f in range(n_f):
        jn_ref[f] = (pooled[f] / cnt_s[f]).astype(jnp.bfloat16)
    jn = jn_ref[...]
    for i in range(k):
        lat = lat + jnp.dot(jn[:, i, :], jw_ref[i * ch:(i + 1) * ch], preferred_element_type=jnp.float32)
    lp_ref[...] = lat
    jn_cp, lt_cp = [], []
    for off in range(1, F):
        jn_cp.append(send(jn_ref, jall_ref.at[f_me], s_jn.at[off - 1], v_jn.at[off - 1],
                          {"frame": lax.rem(f_me + off, F)}))
    for off in range(1, C):
        lt_cp.append(send(lp_ref, latall.at[c_me], s_lt.at[off - 1], v_lt.at[off - 1],
                          {"cam": lax.rem(c_me + off, C)}))
    jall_ref[f_me] = jn
    latall[c_me] = lat

    flying = first
    for s in range(3):
        nxt = []
        for h in range(2):
            rs_recv(halves[h][0][s], flying[h])
            if s < 2:
                nxt.append(rs_send(halves[h][0][s + 1]))
        flying = nxt

    def ag_send(stage):
        start, size, cnt, me, where, buf, s0 = stage
        rows = pl.ds(pl.multiple_of(start + me * size, 16), size)
        return [send(o_ref.at[core, rows], o_ref.at[core, rows], s_ag.at[s0 + off - 1], v_ag.at[s0 + off - 1],
                     where(lax.rem(me + off, cnt))) for off in range(1, cnt)]

    flying = []
    for stages, start, u in halves:
        rows = pl.ds(pl.multiple_of(start, 16), u)
        o_ref[core, rows] = part[core, rows].astype(jnp.bfloat16)
        flying.append(ag_send(stages[2]))
    last = []
    for s in (1, 0, -1):
        nxt = []
        for h in range(2):
            for cp in flying[h]:
                cp.wait_recv()
            if s >= 0:
                nxt.append(ag_send(halves[h][0][s]))
            else:
                rows = pl.ds(0, a_rows) if h == 0 else pl.ds(a_rows, n * u_b)
                last.append(send(o_ref.at[core, rows], o_ref.at[core, rows], s_co.at[3 + h], v_co.at[3 + h],
                                 {"frame": f_me + 1 - 2 * core}))
        flying = nxt
    for cp in lt_cp:
        cp.wait_recv()
    out = latall[0]
    for c in range(1, C):
        out = out + latall[c]
    lat_ref[...] = out
    for cp in ct_cp + jn_cp + last:
        cp.wait_recv()
    for cp in pending:
        cp.wait_send()


def on_device(view_maps, conv_weight, join_weight, valid_cams, latent_grad):
    n_f, n_c, n_r, n_w, ch = view_maps.shape
    feat_len = n_r * n_w * ch
    F, C = lax.axis_size("frame"), lax.axis_size("cam")
    lat_n = join_weight.shape[1]
    n_x, n_y = F // 2, 2
    n_z = C // n_y
    n = n_x * n_y * n_z
    total = 9 * ch
    units = max(2, -(-total // (16 * n)))
    u_a, u_b = -(-units // 2) * 16, units // 2 * 16
    rt = n * (u_a + u_b)
    share = feat_len // C
    k = share // ch
    bf, f32 = jnp.bfloat16, jnp.float32

    count = jnp.sum(valid_cams.astype(f32), axis=1)
    mask = lax.dynamic_slice_in_dim(valid_cams, lax.axis_index("cam") * n_c, n_c, 1).astype(f32)
    wgt = mask / count[:, None]
    jg = jnp.einsum("fl,sl->fs", latent_grad, join_weight, preferred_element_type=f32).astype(bf)
    jg = jg.reshape(n_f, k, ch)

    plan = (F, C, n_x, n_y, n_z, u_a, u_b, n_f, n_c, n_w, ch, k)
    rows = n_f * n_c * n_w
    a1, b1 = n * u_a, n * u_b
    V, D = pltpu.VMEM, pltpu.SemaphoreType.DMA
    n_st = 2 * (n_x + n_y + n_z - 3)
    scratch = [
        V((rows, 6 * ch), bf), V((n_c * n_w, ch), f32), V((n_f, 2, n_c * n_w, ch), f32), V((2, rows, ch), bf),
        V((C, n_f, k, ch), bf), V((n_f, n_r * n_w, ch), f32), V((C, n_f, k, ch), f32), V((C - 1, n_f, k, ch), f32),
        V((2, rt, LANES), f32), V((rt, LANES), bf), V((rt, LANES), bf), V((rt, LANES), bf),
        V((n_x - 1, a1 // n_x, LANES), bf), V((n_y - 1, b1 // n_y, LANES), bf),
        V((n_y - 1, a1 // (n_x * n_y), LANES), bf), V((n_x - 1, b1 // (n_x * n_y), LANES), bf),
        V((n_z - 1, u_a, LANES), bf), V((n_z - 1, u_b, LANES), bf),
        V((n_f, k, ch), bf), V((n_f, lat_n), f32), V((C, n_f, lat_n), f32),
        D((C - 1,)), D((C - 1,)), D((F - 1,)), D((F - 1,)), D((C - 1,)), D((C - 1,)), D((F - 1,)), D((F - 1,)),
        D((C - 1,)), D((C - 1,)), D((5,)), D((5,)), D((n_st,)), D((n_st,)), D((n_st,)), D((n_st,)),
    ]
    vm, sm = pl.BlockSpec(memory_space=pltpu.VMEM), pl.BlockSpec(memory_space=pltpu.SMEM)
    o, latent, jall, call = pl.pallas_call(
        functools.partial(step_kernel, plan),
        out_shape=(jax.ShapeDtypeStruct((2, rt, LANES), bf), jax.ShapeDtypeStruct((n_f, lat_n), f32),
                   jax.ShapeDtypeStruct((F, n_f, k, ch), bf), jax.ShapeDtypeStruct((F, n_f, lat_n), bf)),
        in_specs=[sm, sm, sm, vm, vm, vm, vm, vm],
        out_specs=(vm, vm, vm, vm),
        scratch_shapes=scratch,
        compiler_params=pltpu.CompilerParams(collective_id=0, has_side_effects=True, vmem_limit_bytes=48 << 20),
        name="step",
    )(mask, wgt, count, view_maps, conv_weight.reshape(total, ch), join_weight, jg, latent_grad)

    conv_grad = jnp.concatenate([o[0, :total], o[1, :total]], axis=1).astype(f32).reshape(9, ch, ch)
    sub = share // F
    joined = jall.reshape(F * n_f, share)
    own = lax.dynamic_slice_in_dim(joined, lax.axis_index("frame") * sub, sub, 1)
    join_grad = lax.dot_general(own, call.reshape(F * n_f, lat_n), (((0,), (0,)), ((), ())),
                                preferred_element_type=f32)
    return latent, conv_grad, join_grad


def solution(mesh):
    in_specs = (P("frame", "cam", None, None, None), P(), P("cam", None), P("frame", None), P("frame", None))
    out_specs = (P("frame", None), P(), P(("cam", "frame"), None))
    return jax.shard_map(on_device, mesh=mesh, in_specs=in_specs, out_specs=out_specs, check_vma=False)
```

```python
import functools

import jax
import jax.numpy as jnp
from jax import lax
from jax.experimental import pallas as pl
from jax.experimental.pallas import tpu as pltpu
from jax.sharding import PartitionSpec as P

MESH = pl.DeviceIdType.MESH
LANES = 128
ORDER = "ABA"


def step_kernel(plan, *refs):
    (F, C, n_x, n_y, n_z, u, n_f, n_c, n_w, ch, k) = plan
    (valid_hbm, x_hbm, w_hbm, jw_hbm, cot_hbm,
     o_ref, lat_ref, jall_ref, call_ref,
     valid_s, x_ref, w_ref, jw_ref, cot_ref, s_in, cnt_ref, jgt, jgs,
     z_ref, p_ref, sl_ref, g_ref, jgall, jgf, pool_own, pool_rcv, part, sc, rc, t_ref,
     r1a, r1b, r1c, r2a, r2b, r2c, jnf, jn_ref, lp_ref, latall,
     s_jg, v_jg, s_ct, v_ct, s_pl, v_pl, s_jn, v_jn, s_lt, v_lt, s_co, v_co,
     s_rs, v_rs, s_ag, v_ag, s_cg, v_cg) = refs
    f32, bf = jnp.float32, jnp.bfloat16
    f_me, c_me = lax.axis_index("frame"), lax.axis_index("cam")
    core, x_me = lax.rem(f_me, 2), f_me // 2
    y_me, z_me = lax.rem(c_me, n_y), c_me // n_y
    rows_f = n_c * n_w
    n = n_x * n_y * n_z
    span = n * u
    pending = []

    loads = []
    for i, (src, dst) in enumerate((
            (cot_hbm, cot_ref), (jw_hbm, jw_ref), (x_hbm, x_ref), (w_hbm, w_ref), (valid_hbm, valid_s))):
        loads.append(pltpu.make_async_copy(src, dst, s_in.at[i]))
        loads[-1].start()

    def send(src, dst, ss, rs, where):
        copy = pltpu.make_async_remote_copy(
            src_ref=src, dst_ref=dst, send_sem=ss, recv_sem=rs,
            device_id=where, device_id_type=MESH)
        copy.start()
        pending.append(copy)
        return copy

    plane = [(a, b) for a in range(n_x) for b in range(n_y) if (a, b) != (0, 0)]
    plane.sort(key=lambda t: (t[0] == 0) + (t[1] == 0))

    def plane_at(a, b):
        return lax.rem(x_me + a + n_x, n_x), lax.rem(y_me + b + n_y, n_y)

    def plane_peer(t):
        px, py = plane_at(*t)
        return px * n_y + py, {"frame": px * 2 + core, "cam": z_me * n_y + py}

    def plane_src(t):
        px, py = plane_at(-t[0], -t[1])
        return px * n_y + py

    def line_peer(d):
        v = lax.rem(z_me + d, n_z)
        return v, {"cam": v * n_y + y_me}

    def line_src(d):
        return lax.rem(z_me - d + n_z, n_z)

    xy = (n_x * n_y, x_me * n_y + y_me, plane, plane_peer, plane_src)
    zz = (n_z, z_me, list(range(1, n_z)), line_peer, line_src)

    barrier = pltpu.get_barrier_semaphore()
    met = 0
    for off in range(1, C):
        pl.semaphore_signal(barrier, inc=1, device_id={"cam": lax.rem(c_me + off, C)}, device_id_type=MESH)
        met += 1
    for off in range(1, F):
        pl.semaphore_signal(barrier, inc=1, device_id={"frame": lax.rem(f_me + off, F)}, device_id_type=MESH)
        met += 1
    for t in plane:
        if t[0] and t[1]:
            pl.semaphore_signal(barrier, inc=1, device_id=plane_peer(t)[1], device_id_type=MESH)
            met += 1

    loads[4].wait()
    for f in range(n_f):
        total = valid_s[f, 0]
        for c in range(1, valid_s.shape[1]):
            total = total + valid_s[f, c]
        cnt_ref[f] = jnp.full((1, ch), total.astype(f32), f32)

    loads[0].wait()
    loads[1].wait()
    jgm = lax.dot_general(cot_ref[...], jw_ref[...], (((1,), (1,)), ((), ())), preferred_element_type=f32)
    for i in range(k):
        jgt[:, i, :] = jgm[:, i * ch:(i + 1) * ch]
    jgs[...] = jgt[...].astype(bf)

    loads[2].wait()
    col = lax.rem(lax.broadcasted_iota(jnp.int32, (rows_f, ch), 0), n_w)
    for f in range(n_f):
        for r in range(2):
            xb = x_ref[f, :, r].reshape(rows_f, ch)
            xf = xb.astype(f32)
            lo = jnp.where(col == 0, 0.0, pltpu.roll(xf, 1, 0)).astype(bf)
            hi = jnp.where(col == n_w - 1, 0.0, pltpu.roll(xf, rows_f - 1, 0)).astype(bf)
            rows = pl.ds(f * rows_f, rows_f)
            for dx, piece in enumerate((lo, xb, hi)):
                z_ref[rows, pl.ds((r * 3 + dx) * ch, ch)] = piece
    loads[3].wait()

    def forward(i, carry):
        f, r = i // 2, lax.rem(i, 2)
        row0 = pl.multiple_of(f * rows_f, 16)
        w0 = pl.multiple_of((1 - r) * 3 * ch, 256)
        p_ref[...] = jnp.dot(z_ref[pl.ds(row0, rows_f)], w_ref[pl.ds(w0, 6 * ch)], preferred_element_type=f32)
        inv = 1.0 / cnt_ref[f]
        total = jnp.zeros((n_w, ch), f32)
        for c in range(n_c):
            on = valid_s[f, c_me * n_c + c].astype(f32)
            pre = p_ref[pl.ds(c * n_w, n_w)]
            sig = jax.nn.sigmoid(pre)
            feat = (pre * sig).astype(bf).astype(f32)
            total = total + on * feat
            sl_ref[f, r, pl.ds(c * n_w, n_w)] = (on * inv) * (sig * (1.0 + pre * (1.0 - sig)))
        jgf[f, pl.ds(pl.multiple_of(r * n_w, n_w), n_w)] = total
        return carry

    pl.semaphore_wait(barrier, met)
    jgall[c_me] = jgs[...]
    jg_cp = []
    for off in range(1, C):
        jg_cp.append(send(jgs, jgall.at[c_me], s_jg.at[off - 1], v_jg.at[off - 1],
                          {"cam": lax.rem(c_me + off, C)}))
    lax.fori_loop(0, 2 * n_f, forward, 0)
    for c in range(C):
        for f in range(n_f):
            pool_own[c, f] = jgf[f, c * k:(c + 1) * k]
    pl_cp = []
    for off in range(1, C):
        to = lax.rem(c_me + off, C)
        pl_cp.append(send(pool_own.at[to], pool_rcv.at[off - 1], s_pl.at[off - 1], v_pl.at[off - 1], {"cam": to}))

    for cp in jg_cp:
        cp.wait_recv()
    for c in range(C):
        for f in range(n_f):
            jgf[f, c * k:(c + 1) * k] = jgall[c, f].astype(f32)
    for f in range(n_f):
        for r in range(2):
            jg = jgf[f, r * n_w:(r + 1) * n_w]
            for c in range(n_c):
                g = (jg * sl_ref[f, r, pl.ds(c * n_w, n_w)]).astype(bf)
                g_ref[r, pl.ds(f * rows_f + c * n_w, n_w)] = g

    third = 3 * ch
    if span > third:
        for b in range(3):
            part[:, b * span + third:(b + 1) * span] = jnp.zeros((2, span - third, LANES), f32)
    co_cp = []

    def dot_t(lane0, r):
        return lax.dot_general(z_ref[:, lane0:lane0 + third], g_ref[r], (((0,), (0,)), ((), ())),
                               preferred_element_type=f32)

    def backward(b):
        if b == 0:
            val = dot_t(0, 1)
        elif b == 1:
            val = dot_t(0, 0) + dot_t(third, 1)
        else:
            val = dot_t(third, 0)
        rows = pl.ds(b * span, third)
        part[0, rows] = val[:, :LANES]
        part[1, rows] = val[:, LANES:]
        sc[rows] = part[1 - core, rows].astype(bf)
        co_cp.append(send(sc.at[rows], rc.at[rows], s_co.at[b], v_co.at[b], {"frame": f_me + 1 - 2 * core}))

    def pair_sum(b):
        co_cp[b].wait_recv()
        rows = pl.ds(b * span, third)
        part[core, rows] = part[core, rows] + rc[rows].astype(f32)

    streams = []
    sem_at = 0
    kinds = {"A": (xy, zz), "B": (zz, xy)}
    for b, bufs in enumerate(((r1a, r2a), (r1b, r2b), (r1c, r2c))):
        start, size, stages = b * span, span, []
        for group, buf in zip(kinds[ORDER[b]], bufs):
            size = size // group[0]
            stages.append((start, size, group, buf, sem_at))
            start = start + group[1] * size
            sem_at += group[0] - 1
        streams.append((stages, start))

    def block(start, index, size):
        return pl.ds(pl.multiple_of(start + index * size, 8), size)

    def rs_send(stage):
        start, size, (cnt, me, offs, peer, source), buf, s0 = stage
        out = []
        for i, off in enumerate(offs):
            v, where = peer(off)
            rows = block(start, v, size)
            t_ref[rows] = part[core, rows].astype(bf)
            out.append(send(t_ref.at[rows], buf.at[i], s_rs.at[s0 + i], v_rs.at[s0 + i], where))
        return out

    def rs_recv(stage, cps):
        start, size, (cnt, me, offs, peer, source), buf, s0 = stage
        rows = block(start, me, size)
        for cp in cps:
            cp.wait_recv()
        acc = part[core, rows]
        for i in range(len(cps)):
            acc = acc + buf[i].astype(f32)
        part[core, rows] = acc

    fly = [None] * 3
    backward(0)
    backward(1)
    pair_sum(0)
    fly[0] = rs_send(streams[0][0][0])
    backward(2)
    pair_sum(1)
    fly[1] = rs_send(streams[1][0][0])
    pair_sum(2)
    fly[2] = rs_send(streams[2][0][0])

    for cp in pl_cp:
        cp.wait_recv()
    pooled = pool_own[c_me]
    for off in range(C - 1):
        pooled = pooled + pool_rcv[off]
    for f in range(n_f):
        val = pooled[f] / cnt_ref[f]
        for i in range(k):
            jnf[i, f:f + 1] = val[i:i + 1]
    jn_ref[...] = jnf[...].astype(bf)
    lat = jnp.zeros((n_f, jw_ref.shape[1]), f32)
    for i in range(k):
        lat = lat + jnp.dot(jn_ref[i], jw_ref[i * ch:(i + 1) * ch], preferred_element_type=f32)
    lp_ref[...] = lat
    jn_cp, lt_cp, ct_cp = [], [], []
    for off in range(1, F):
        to = {"frame": lax.rem(f_me + off, F)}
        jn_cp.append(send(jn_ref, jall_ref.at[f_me], s_jn.at[off - 1], v_jn.at[off - 1], to))
        ct_cp.append(send(cot_ref, call_ref.at[f_me], s_ct.at[off - 1], v_ct.at[off - 1], to))
    for off in range(1, C):
        lt_cp.append(send(lp_ref, latall.at[c_me], s_lt.at[off - 1], v_lt.at[off - 1],
                          {"cam": lax.rem(c_me + off, C)}))
    jall_ref[f_me] = jn_ref[...]
    call_ref[f_me] = cot_ref[...]
    latall[c_me] = lat

    for b in range(3):
        rs_recv(streams[b][0][0], fly[b])
        fly[b] = rs_send(streams[b][0][1])

    def ag_send(stage):
        start, size, (cnt, me, offs, peer, source), buf, s0 = stage
        rows = block(start, me, size)
        return [send(o_ref.at[core, rows], o_ref.at[core, rows], s_ag.at[s0 + i], v_ag.at[s0 + i], peer(off)[1])
                for i, off in enumerate(offs)]

    def finish(h):
        stages, start = streams[h]
        rows = block(start, 0, u)
        o_ref[core, rows] = part[core, rows].astype(bf)
        return ag_send(stages[1])

    last = []

    def to_pair(rows):
        i = len(last)
        last.append(send(o_ref.at[core, rows], o_ref.at[core, rows], s_cg.at[i], v_cg.at[i],
                         {"frame": f_me + 1 - 2 * core}))

    for b in range(3):
        rs_recv(streams[b][0][1], fly[b])
        fly[b] = finish(b)
    outer = []
    for b in range(3):
        for cp in fly[b]:
            cp.wait_recv()
        stage = streams[b][0][0]
        outer.append(ag_send(stage))
        to_pair(block(stage[0], stage[2][1], stage[1]))
    for cp in lt_cp:
        cp.wait_recv()
    out = latall[0]
    for c in range(1, C):
        out = out + latall[c]
    lat_ref[...] = out
    for cp in ct_cp + jn_cp:
        cp.wait_recv()
    for h in range(3):
        start, size, (cnt, me, offs, peer, source), buf, s0 = streams[h][0][0]
        order = list(range(len(offs)))[::-1]
        for i in order:
            outer[h][i].wait_recv()
            to_pair(block(start, source(offs[i]), size))
    for cp in last:
        cp.wait_recv()
    for cp in pending:
        cp.wait_send()


def tail_kernel(sub, o_ref, lat_ref, jall_ref, call_ref, lat_hbm, conv_hbm, join_hbm, cbuf, jbuf, jx, cx, sem):
    taps, ch, lat_n = cbuf.shape[0], cbuf.shape[1], cx.shape[1]
    F, k, n_f, _ = jall_ref.shape
    span = o_ref.shape[1] // 3
    copies = [pltpu.make_async_copy(lat_ref, lat_hbm, sem.at[0])]
    copies[0].start()
    for t in range(taps):
        for half in range(2):
            cbuf[t, :, half * LANES:(half + 1) * LANES] = o_ref[half, pl.ds(t // 3 * span + t % 3 * ch, ch)].astype(jnp.float32)
        copies.append(pltpu.make_async_copy(cbuf.at[t], conv_hbm.at[t], sem.at[1 + t]))
        copies[-1].start()
    first = lax.axis_index("frame") * sub
    for g in range(F):
        cx[g * n_f:(g + 1) * n_f] = call_ref[g].astype(jnp.float32)
    cot = cx[...].astype(jnp.bfloat16)
    for j in range(max(1, sub // ch)):
        for g in range(F):
            jx[g * n_f:(g + 1) * n_f] = jall_ref[g, first // ch + j].astype(jnp.float32)
        jbuf[j * ch:(j + 1) * ch] = lax.dot_general(jx[...].astype(jnp.bfloat16), cot, (((0,), (0,)), ((), ())),
                                                    preferred_element_type=jnp.float32)
    rows = pl.ds(pl.multiple_of(lax.rem(first, ch), 8), sub)
    copies.append(pltpu.make_async_copy(jbuf.at[rows], join_hbm, sem.at[1 + taps]))
    copies[-1].start()
    for cp in copies:
        cp.wait()


def on_device(view_maps, conv_weight, join_weight, valid_cams, latent_grad):
    n_f, n_c, n_r, n_w, ch = view_maps.shape
    feat_len = n_r * n_w * ch
    F, C = lax.axis_size("frame"), lax.axis_size("cam")
    lat_n = join_weight.shape[1]
    n_x, n_y = F // 2, 2
    n_z = C // n_y
    n = n_x * n_y * n_z
    taps = conv_weight.shape[0]
    total = taps * ch
    u = -(-total // (24 * n)) * 8
    span = n * u
    rt = 3 * span
    share = feat_len // C
    k = share // ch
    bf, f32 = jnp.bfloat16, jnp.float32

    plan = (F, C, n_x, n_y, n_z, u, n_f, n_c, n_w, ch, k)
    rows = n_f * n_c * n_w
    n_p = n_x * n_y
    V, D = pltpu.VMEM, pltpu.SemaphoreType.DMA
    n_st = 3 * (n_p + n_z - 2)
    groups = [(n_p, n_z) if kind == "A" else (n_z, n_p) for kind in ORDER]
    scratch = [
        pltpu.SMEM(valid_cams.shape, jnp.int32), V(view_maps.shape, bf), V((total, ch), bf), V(join_weight.shape, bf), V((n_f, lat_n), bf), D((5,)),
        V((n_f, 1, ch), f32), V((n_f, k, ch), f32), V((n_f, k, ch), bf),
        V((rows, 6 * ch), bf), V((n_c * n_w, ch), f32), V((n_f, 2, n_c * n_w, ch), f32), V((2, rows, ch), bf),
        V((C, n_f, k, ch), bf), V((n_f, n_r * n_w, ch), f32), V((C, n_f, k, ch), f32), V((C - 1, n_f, k, ch), f32),
        V((2, rt, LANES), f32), V((rt, LANES), bf), V((rt, LANES), bf), V((rt, LANES), bf),
        *[V((g[0] - 1, span // g[0], LANES), bf) for g in groups], *[V((g[1] - 1, u, LANES), bf) for g in groups],
        V((k, n_f, ch), f32), V((k, n_f, ch), bf), V((n_f, lat_n), f32), V((C, n_f, lat_n), f32),
        D((C - 1,)), D((C - 1,)), D((F - 1,)), D((F - 1,)), D((C - 1,)), D((C - 1,)), D((F - 1,)), D((F - 1,)),
        D((C - 1,)), D((C - 1,)), D((3,)), D((3,)), D((n_st,)), D((n_st,)), D((n_st,)), D((n_st,)),
        D((3 * (n_p + n_z),)), D((3 * (n_p + n_z),)),
    ]
    vm = pl.BlockSpec(memory_space=pltpu.VMEM)
    hbm = pl.BlockSpec(memory_space=pltpu.HBM)
    o, lat, jall, call = pl.pallas_call(
        functools.partial(step_kernel, plan),
        out_shape=(jax.ShapeDtypeStruct((2, rt, LANES), bf), jax.ShapeDtypeStruct((n_f, lat_n), f32),
                   jax.ShapeDtypeStruct((F, k, n_f, ch), bf), jax.ShapeDtypeStruct((F, n_f, lat_n), bf)),
        in_specs=[hbm, hbm, hbm, hbm, hbm],
        out_specs=(vm, vm, vm, vm),
        scratch_shapes=scratch,
        compiler_params=pltpu.CompilerParams(collective_id=0, has_side_effects=True, vmem_limit_bytes=48 << 20),
        name="step",
    )(*(pltpu.with_memory_space_constraint(a, pltpu.HBM)
                    for a in (valid_cams, view_maps, conv_weight.reshape(total, ch), join_weight, latent_grad)))

    sub = share // F
    return pl.pallas_call(
        functools.partial(tail_kernel, sub),
        out_shape=(jax.ShapeDtypeStruct((n_f, lat_n), f32), jax.ShapeDtypeStruct((taps, ch, ch), f32),
                   jax.ShapeDtypeStruct((sub, lat_n), f32)),
        in_specs=[vm, vm, vm, vm],
        out_specs=(hbm, hbm, hbm),
        scratch_shapes=[V((taps, ch, ch), f32), V((max(ch, sub), lat_n), f32), V((F * n_f, ch), f32),
                        V((F * n_f, lat_n), f32), D((taps + 2,))],
        compiler_params=pltpu.CompilerParams(vmem_limit_bytes=16 << 20),
        name="tail",
    )(o, lat, jall, call)


def solution(mesh):
    in_specs = (P("frame", "cam", None, None, None), P(), P("cam", None), P("frame", None), P("frame", None))
    out_specs = (P("frame", None), P(), P(("cam", "frame"), None))
    return jax.shard_map(on_device, mesh=mesh, in_specs=in_specs, out_specs=out_specs, check_vma=False)
```
